128 devices in a mesh: pipe: 4 (over z_hi, core), tensor: 8 (over z_lo, y), dp: 4 (over x).
Axes of the slice: x: 4, y: 4, z: 4 (z_hi: 2, z_lo: 2; z = z_hi * 2 + z_lo), core: 2. Of those that a mesh axis runs over, the one named last changes fastest.
Arguments:
- tokens: bfloat16 [4, 1024, 4096], P('pipe', ('tensor', 'dp')), may hold values from -6 to 6
- grad_out: bfloat16 [4, 1024, 4096], P('pipe', ('tensor', 'dp')), may hold values from -6 to 6
- weights_in: bfloat16 [4, 2, 14336, 4096], P('pipe', None, ('tensor', 'dp')), may hold values from -0.09375 to 0.09375
- weights_down: bfloat16 [4, 14336, 4096], P('pipe', ('tensor', 'dp')), may hold values from -0.046875 to 0.046875
- projector: bfloat16 [4, 4096, 512], P('pipe'), may hold values from -0.25 to 0.25
- moment_first: float32 [4, 14336, 512], P('pipe', ('tensor', 'dp')), may hold values from -60 to 60
- moment_second: float32 [4, 14336, 512], P('pipe', ('tensor', 'dp')), may hold values from 1 to 10
Outputs:
- grad_prev: bfloat16 [4, 1024, 4096], P('pipe', ('tensor', 'dp'))
- update: bfloat16 [4, 14336, 4096], P('pipe', ('tensor', 'dp'))
The draws below stay inside these ranges and needn't reach their ends.
All inputs are finite; a program needn't handle non-finite values.
Results may differ from the reference program's by a relative error of at most 0.0064.
Values may be sent and summed in bfloat16 or wider, within the bound.
A program may use at most 128 MiB of HBM per device.

```python
import math
import jax
import jax.numpy as jnp

D = 4096
FF = 14336
RANK = 512
TOKENS = 1024
N_PIPE = 4


def level_of(rng, shape, pieces, smallest, largest):
    level = 1.0
    for dim, shards_of in pieces:
        steps = jax.random.uniform(jax.random.fold_in(jax.random.fold_in(rng, 6), dim), (shards_of,), jnp.float32, smallest / len(pieces), largest / len(pieces))
        level = level * jnp.repeat(jnp.exp(steps), shape[dim] // shards_of).reshape((-1,) + (1,) * (len(shape) - 1 - dim))
    return level


def bell_draw(key, shape, width, limit, cuts=(), dtype=jnp.bfloat16):
    loudness = level_of(key, shape, cuts, -0.22, 0.18) if cuts else 1.0
    entries = jax.random.normal(key, shape, jnp.float32) * width * loudness
    return jnp.minimum(jnp.maximum(entries, -limit), limit).astype(dtype)


def setup_inputs(seed: int = 0) -> dict:
    keys = jax.random.split(jax.random.key(seed), 8)
    tokens = bell_draw(keys[0], (N_PIPE, TOKENS, D), 1.0, 6.0, ((0, 4), (1, 32)))
    grad_out = bell_draw(keys[1], (N_PIPE, TOKENS, D), 1.0, 6.0, ((0, 4), (1, 32)))
    weights_in = bell_draw(keys[2], (N_PIPE, 2, FF, D), D ** -0.5, 0.09375, ((0, 4), (2, 32)))
    weights_down = bell_draw(keys[3], (N_PIPE, FF, D), FF ** -0.5, 0.046875, ((0, 4), (1, 32)))
    projector = bell_draw(keys[4], (N_PIPE, D, RANK), RANK ** -0.5, 0.25, ((0, 4),))
    moment_first = bell_draw(keys[5], (N_PIPE, FF, RANK), 10.0, 60.0, ((0, 4), (1, 32)), jnp.float32)
    moment_second = jnp.clip(jnp.exp(math.log(10.0) - 2.3025851 * jax.random.uniform(keys[6], (N_PIPE, FF, RANK), jnp.float32) ** level_of(keys[6], (N_PIPE, FF, RANK), ((0, 4), (1, 32)), -0.2, 0.2)), 1.0, 10.0)
    return dict(tokens=tokens, grad_out=grad_out, weights_in=weights_in, weights_down=weights_down, projector=projector, moment_first=moment_first, moment_second=moment_second)


beta_one = 0.9
beta_two = 0.999
bias_one = 1.0 - 0.9 ** 10
bias_two = 1.0 - 0.999 ** 10
epsilon = 1e-08

def adam_update(low_grad, moment_first, moment_second, projector):
    first_moment = beta_one * moment_first + (1.0 - beta_one) * low_grad
    second_moment = beta_two * moment_second + (1.0 - beta_two) * low_grad * low_grad
    normed = (first_moment / bias_one / (jnp.sqrt(second_moment / bias_two) + epsilon)).astype(jnp.bfloat16)
    return jnp.dot(normed, projector.T, preferred_element_type=jnp.float32).astype(jnp.bfloat16)

def section_backward(tokens, grad_out, weights_in, weights_down, projector, moment_first, moment_second):
    gate_pre = jnp.dot(weights_in[0], tokens.T, preferred_element_type=jnp.float32)
    up_act = jnp.dot(weights_in[1], tokens.T, preferred_element_type=jnp.float32)
    sigmoid_gate = jax.nn.sigmoid(gate_pre)
    silu_gate = gate_pre * sigmoid_gate
    hidden = (silu_gate * up_act).astype(jnp.bfloat16)
    grad_hidden = jnp.dot(weights_down, grad_out.T, preferred_element_type=jnp.float32)
    grad_gate = (grad_hidden * up_act * sigmoid_gate * (1.0 + gate_pre * (1.0 - sigmoid_gate))).astype(jnp.bfloat16)
    grad_up = (grad_hidden * silu_gate).astype(jnp.bfloat16)
    grad_in = jnp.dot(grad_gate.T, weights_in[0], preferred_element_type=jnp.float32)
    grad_in = grad_in + jnp.dot(grad_up.T, weights_in[1], preferred_element_type=jnp.float32)
    grad_proj = jnp.dot(grad_out, projector, preferred_element_type=jnp.float32).astype(jnp.bfloat16)
    low_grad = jnp.dot(hidden, grad_proj, preferred_element_type=jnp.float32)
    update = adam_update(low_grad, moment_first, moment_second, projector)
    return (grad_in, update)

def reference(tokens, grad_out, weights_in, weights_down, projector, moment_first, moment_second):
    input_grads = []
    updates = []
    for layer_index in range(N_PIPE):
        grad_in, update = section_backward(tokens[layer_index], grad_out[layer_index], weights_in[layer_index], weights_down[layer_index], projector[layer_index], moment_first[layer_index], moment_second[layer_index])
        input_grads.append(grad_in)
        updates.append(update)
    grad_prev = jnp.roll(jnp.stack(input_grads), -1, axis=0).astype(jnp.bfloat16)
    return (grad_prev, jnp.stack(updates))
```

```python
import functools

import jax
import jax.numpy as jnp
from jax import lax
from jax.experimental import pallas as pl
from jax.experimental.pallas import tpu as pltpu
from jax.sharding import PartitionSpec as P

beta_one = 0.9
beta_two = 0.999
bias_one = 1.0 - 0.9**10
bias_two = 1.0 - 0.999**10
epsilon = 1e-08

MESH = pl.DeviceIdType.MESH
bf16, f32 = jnp.bfloat16, jnp.float32
D, FF, RANK = 4096, 448, 512
ROWS = 16
C1 = 2816
S1 = 2816
CT = 1024
UT = 1024
NT = (((1,), (1,)), ((), ()))
NN = (((1,), (0,)), ((), ()))


def dot(a, b, dims=NN):
    return lax.dot_general(a, b, dims, preferred_element_type=f32)


def kernel(tok, grd, win, wdn, prj, mom1, mom2, out_prev, out_upd,
           buf, WI, WD, PR, M1, M2, part, R1, R2o, R2, R3o, R3, R4,
           GA, UA, HI, GT, TA, PC, LG, NM, US,
           lsem, wsem, usem, recv, sent):
    pipe = lax.axis_index("pipe")
    t = lax.axis_index("tensor")
    x = lax.axis_index("dp")
    z0, y = t // 4, t % 4
    z1 = 1 - z0
    Z = (z0, z1)
    L0, M0 = (y, x), (x, y)

    def dev(h, l, m, z):
        return {"tensor": z * 4 + (l if h == 0 else m), "dp": m if h == 0 else l}

    def to(v, d):
        return (v + 1 + 2 * d) % 4

    def frm(v, d):
        return (v + 3 + 2 * d) % 4

    def ldev(h, d):
        return dev(h, to(L0[h], d), M0[h], z0)

    def mdev(h, d):
        return dev(h, L0[h], to(M0[h], d), z0)

    zdev = dev(0, L0[0], M0[0], z1)
    pdev = {"pipe": (pipe + 3) % 4}
    barrier = pltpu.get_barrier_semaphore()
    for h in (0, 1):
        for d in (0, 1):
            pl.semaphore_signal(barrier, inc=1, device_id=ldev(h, d), device_id_type=MESH)
    pl.semaphore_signal(barrier, inc=1, device_id=zdev, device_id_type=MESH)
    for step in (1, 3):
        pl.semaphore_signal(
            barrier, inc=1, device_id={"pipe": (pipe + step) % 4}, device_id_type=MESH
        )

    own = [
        pltpu.make_async_copy(
            src.at[0, h * ROWS : (h + 1) * ROWS, :],
            buf.at[h, L0[h], z0, M0[h], a],
            lsem.at[h, a],
        )
        for h in (0, 1)
        for a, src in ((0, tok), (1, grd))
    ]
    for c in own:
        c.start()
    loads = [
        pltpu.make_async_copy(src.at[0], dst, wsem.at[i])
        for i, (src, dst) in enumerate(((win, WI), (wdn, WD), (prj, PR), (mom1, M1), (mom2, M2)))
    ]
    for c in loads:
        c.start()
    LG[...] = jnp.zeros_like(LG)
    for c in own:
        c.wait()
    pl.semaphore_wait(barrier, 7)

    pending = []

    def send(src, dst, name, idx, to_dev):
        c = pltpu.make_async_remote_copy(
            src, dst, sent[name].at[idx], recv[name].at[idx], device_id=to_dev, device_id_type=MESH
        )
        c.start()
        pending.append(c)

    def arrive(ref, name, idx):
        pltpu.make_async_remote_copy(
            ref, ref, sent[name].at[idx], recv[name].at[idx], device_id=zdev, device_id_type=MESH
        ).wait_recv()

    def rot(v, r):
        return (v + r) % 4

    def cols(zz, edge):
        return (0, D) if zz == 0 else (0, edge)

    def half(zz, d, edge):
        n = cols(zz, edge)[1] // 2
        return (0, n) if d == 0 else (n, 2 * n)

    def piece(h, l, zz, m, c):
        return buf.at[h, l, Z[zz], m, :, :, c[0] : c[1]]

    def gsend(h, l, zz, m, c, name, idx, to_dev):
        r = piece(h, l, zz, m, c)
        send(r, r, name, idx, to_dev)

    def l_spread(h, zz, mr):
        for d in (0, 1):
            gsend(h, L0[h], zz, rot(M0[h], mr), cols(zz, C1), "gl", (h, zz, mr, d), ldev(h, d))

    def m_spread(h, zz):
        for d in (0, 1):
            gsend(h, L0[h], zz, M0[h], cols(zz, C1), "gm", (h, zz, d), mdev(h, d))

    def z_forward(h, lr, mr):
        gsend(h, rot(L0[h], lr), 0, rot(M0[h], mr), (C1, D), "gy", (h, lr, mr), zdev)

    def on_m(zz):
        for h in (0, 1):
            for d in (0, 1):
                o = frm(M0[h], d)
                arrive(piece(h, L0[h], zz, o, cols(zz, C1)), "gm", (h, zz, d))
                gsend(h, L0[h], zz, o, half(zz, d, C1), "gmo", (h, zz, d), mdev(h, d))
                l_spread(h, zz, 3 - 2 * d)
                if zz == 0:
                    z_forward(h, 0, 3 - 2 * d)

    def on_mo(zz):
        for h in (0, 1):
            for d in (0, 1):
                arrive(
                    piece(h, L0[h], zz, rot(M0[h], 2), half(zz, d, C1)), "gmo", (h, zz, d)
                )
            l_spread(h, zz, 2)
            if zz == 0:
                z_forward(h, 0, 2)

    def on_z():
        for h in (0, 1):
            arrive(piece(h, L0[h], 1, M0[h], (0, D)), "gz", (h,))
            m_spread(h, 1)
            l_spread(h, 1, 0)

    def on_l(zz, mr):
        for h in (0, 1):
            m = rot(M0[h], mr)
            for d in (0, 1):
                o = frm(L0[h], d)
                arrive(piece(h, o, zz, m, cols(zz, C1)), "gl", (h, zz, mr, d))
                gsend(h, o, zz, m, half(zz, d, C1), "glo", (h, zz, mr, d), ldev(h, d))
                if zz == 0:
                    z_forward(h, 3 - 2 * d, mr)

    def on_lo(zz, mr):
        for h in (0, 1):
            m = rot(M0[h], mr)
            for d in (0, 1):
                arrive(
                    piece(h, rot(L0[h], 2), zz, m, half(zz, d, C1)), "glo", (h, zz, mr, d)
                )
            if zz == 0:
                z_forward(h, 2, mr)

    def on_y(lr, mrs):
        for mr in mrs:
            for h in (0, 1):
                arrive(
                    piece(h, rot(L0[h], lr), 1, rot(M0[h], mr), (C1, D)), "gy", (h, lr, mr)
                )

    def rows_of(lr, a):
        return jnp.concatenate(
            [buf[h, rot(L0[h], lr), :, :, a].reshape(8 * ROWS, D) for h in (0, 1)], 0
        )

    def t_gate(lr):
        GA[...] = dot(WI[0], rows_of(lr, 0), NT)

    def t_up(lr):
        UA[...] = dot(WI[1], rows_of(lr, 0), NT)

    def t_act(lr):
        gh = dot(WD[...], rows_of(lr, 1), NT)
        g, u = GA[...], UA[...]
        s = 1.0 / (1.0 + jnp.exp(-g))
        silu = g * s
        HI[...] = (silu * u).astype(bf16)
        GT[0] = (gh * u * s * (1.0 + g * (1.0 - s))).astype(bf16)
        GT[1] = (gh * silu).astype(bf16)

    def t_turn(lr):
        TA[0] = GT[0].T
        TA[1] = GT[1].T

    def t_low(lr):
        PC[...] = dot(rows_of(lr, 1), PR[...]).astype(bf16)
        LG[...] += dot(HI[...], PC[...])

    def t_in(lr, j):
        c = slice(j * CT, (j + 1) * CT)
        r = (dot(TA[0], WI[0, :, c]) + dot(TA[1], WI[1, :, c])).astype(bf16)
        for h in (0, 1):
            part[h, rot(L0[h], lr), :, :, :, c] = r[h * 128 : (h + 1) * 128].reshape(
                2, 4, ROWS, CT
            )

    def pview(h, l, zz, m, c):
        return part.at[h, l, Z[zz], m, :, c[0] : c[1]]

    def add(h, l, zz, m, c, *refs):
        v = pview(h, l, zz, m, c)
        total = v[...].astype(f32)
        for r in refs:
            total += r[...].astype(f32)
        v[...] = total.astype(bf16)

    def y_send(lr):
        for h in (0, 1):
            for mr in range(4):
                l, m = rot(L0[h], lr), rot(M0[h], mr)
                send(pview(h, l, 1, m, (S1, D)), R1.at[h, lr, mr], "ry", (h, lr, mr), zdev)

    def y_add(lr, mr):
        for h in (0, 1):
            l, m = rot(L0[h], lr), rot(M0[h], mr)
            r = R1.at[h, lr, mr]
            arrive(r, "ry", (h, lr, mr))
            add(h, l, 0, m, (S1, D), r)

    def lo_send(zz, mr, d):
        for h in (0, 1):
            c = half(zz, d, S1)
            n = c[1] - c[0]
            v = pview(h, rot(L0[h], 2), zz, rot(M0[h], mr), c)
            send(v, R2o.at[h, zz, mr, d, :, 0:n], "rlo", (h, zz, mr, d), ldev(h, d))

    def lo_add(zz, mr):
        for h in (0, 1):
            for d in (0, 1):
                c = half(zz, d, S1)
                r = R2o.at[h, zz, mr, d, :, 0 : c[1] - c[0]]
                arrive(r, "rlo", (h, zz, mr, d))
                l, m = to(L0[h], d), rot(M0[h], mr)
                add(h, l, zz, m, c, r)
                f = cols(zz, S1)
                send(
                    pview(h, l, zz, m, f),
                    R2.at[h, zz, mr, d, :, 0 : f[1]],
                    "rl",
                    (h, zz, mr, d),
                    ldev(h, d),
                )

    def l_add(zz, mr):
        f = cols(zz, S1)
        for h in (0, 1):
            rs = [R2.at[h, zz, mr, d, :, 0 : f[1]] for d in (0, 1)]
            for d in (0, 1):
                arrive(rs[d], "rl", (h, zz, mr, d))
            add(h, L0[h], zz, rot(M0[h], mr), f, *rs)

    def mo_send(zz):
        for h in (0, 1):
            for d in (0, 1):
                c = half(zz, d, S1)
                v = pview(h, L0[h], zz, rot(M0[h], 2), c)
                send(v, R3o.at[h, zz, d, :, 0 : c[1] - c[0]], "rmo", (h, zz, d), mdev(h, d))

    def mo_add(zz, d):
        for h in (0, 1):
            c, f = half(zz, d, S1), cols(zz, S1)
            r = R3o.at[h, zz, d, :, 0 : c[1] - c[0]]
            arrive(r, "rmo", (h, zz, d))
            m = to(M0[h], d)
            add(h, L0[h], zz, m, c, r)
            send(
                pview(h, L0[h], zz, m, f),
                R3.at[h, zz, d, :, 0 : f[1]],
                "rm",
                (h, zz, d),
                mdev(h, d),
            )

    def m_add(zz):
        f = cols(zz, S1)
        for h in (0, 1):
            rs = [R3.at[h, zz, d, :, 0 : f[1]] for d in (0, 1)]
            for d in (0, 1):
                arrive(rs[d], "rm", (h, zz, d))
            add(h, L0[h], zz, M0[h], f, *rs)

    def z_send():
        for h in (0, 1):
            send(pview(h, L0[h], 1, M0[h], (0, S1)), R4.at[h], "rz", (h,), zdev)

    def z_add():
        for h in (0, 1):
            arrive(R4.at[h], "rz", (h,))
            add(h, L0[h], 0, M0[h], (0, S1), R4.at[h])
            send(
                pview(h, L0[h], 0, M0[h], (0, D)),
                out_prev.at[0, h * ROWS : (h + 1) * ROWS, :],
                "out",
                (h,),
                pdev,
            )

    def adam():
        low = LG[...]
        first = beta_one * M1[...] + (1.0 - beta_one) * low
        second = beta_two * M2[...] + (1.0 - beta_two) * low * low
        NM[...] = (first / bias_one / (jnp.sqrt(second / bias_two) + epsilon)).astype(bf16)

    def u_copy(j):
        return pltpu.make_async_copy(
            US.at[j % 2], out_upd.at[0, :, j * UT : (j + 1) * UT], usem.at[j % 2]
        )

    def update(j):
        if j >= 2:
            u_copy(j - 2).wait()
        US[j % 2] = dot(NM[...], PR[j * UT : (j + 1) * UT, :], NT).astype(bf16)
        u_copy(j).start()

    for h in (0, 1):
        gsend(h, L0[h], 0, M0[h], (0, D), "gz", (h,), zdev)
        m_spread(h, 0)
    for h in (0, 1):
        l_spread(h, 0, 0)
    on_m(0)
    on_z()
    on_l(0, 0)
    on_mo(0)
    on_m(1)
    on_l(0, 3)
    on_l(0, 1)
    on_mo(1)
    on_lo(0, 0)
    on_y(0, (3, 1, 2))
    for c in loads:
        c.wait()
    t_gate(0)
    on_l(0, 2)
    t_up(0)
    on_l(1, 0)
    t_act(0)
    t_turn(0)
    on_l(1, 3)
    t_low(0)
    on_l(1, 1)
    t_in(0, 0)
    t_in(0, 1)
    on_lo(0, 3)
    t_in(0, 2)
    t_in(0, 3)
    on_lo(0, 1)
    on_l(1, 2)
    on_lo(0, 2)
    on_y(3, range(4))
    for lr, more in ((3, (0, 3)), (1, (1, 2))):
        if lr == 1:
            on_y(1, range(4))
        t_gate(lr)
        t_up(lr)
        t_act(lr)
        on_lo(1, more[0])
        t_turn(lr)
        t_low(lr)
        t_in(lr, 0)
        t_in(lr, 1)
        on_lo(1, more[1])
        t_in(lr, 2)
        t_in(lr, 3)
    on_y(2, range(4))
    for lr in (3, 1, 0):
        y_send(lr)
    t_gate(2)
    t_up(2)
    t_act(2)
    t_turn(2)
    for j in range(4):
        t_in(2, j)
    y_send(2)
    for mr in (2, 3, 1, 0):
        lo_send(1, mr, 0)
        lo_send(1, mr, 1)
        lo_send(0, mr, 0)
    t_low(2)
    for mr in (2, 3, 1, 0):
        y_add(2, mr)
        lo_send(0, mr, 1)
    adam()
    for mr in (2, 3, 1, 0):
        y_add(3, mr)
        y_add(1, mr)
        lo_add(1, mr)
        lo_add(0, mr)
        y_add(0, mr)
        update((2, 3, 1, 0).index(mr))
    for mr in (2, 3, 1, 0):
        for zz in (1, 0):
            l_add(zz, mr)
            if mr == 2:
                mo_send(zz)
            elif mr != 0:
                mo_add(zz, 0 if mr == 1 else 1)
    m_add(1)
    z_send()
    m_add(0)
    z_add()
    for j in (2, 3):
        u_copy(j).wait()
    for h in (0, 1):
        arrive(out_prev.at[0, h * ROWS : (h + 1) * ROWS, :], "out", (h,))
    for c in pending:
        c.wait_send()


SEMAPHORES = {
    "gz": (2,),
    "gm": (2, 2, 2),
    "gmo": (2, 2, 2),
    "gl": (2, 2, 4, 2),
    "glo": (2, 2, 4, 2),
    "gy": (2, 4, 4),
    "ry": (2, 4, 4),
    "rlo": (2, 2, 4, 2),
    "rl": (2, 2, 4, 2),
    "rmo": (2, 2, 2),
    "rm": (2, 2, 2),
    "rz": (2,),
    "out": (2,),
}


def per_device(*args):
    dma = pltpu.SemaphoreType.DMA
    vmem = pltpu.VMEM
    return pl.pallas_call(
        kernel,
        out_shape=(
            jax.ShapeDtypeStruct((1, 2 * ROWS, D), bf16),
            jax.ShapeDtypeStruct((1, FF, D), bf16),
        ),
        in_specs=[pl.BlockSpec(memory_space=pl.ANY)] * 7,
        out_specs=[pl.BlockSpec(memory_space=pl.ANY)] * 2,
        scratch_shapes=[
            vmem((2, 4, 2, 4, 2, ROWS, D), bf16),
            vmem((2, FF, D), bf16),
            vmem((FF, D), bf16),
            vmem((D, RANK), bf16),
            vmem((FF, RANK), f32),
            vmem((FF, RANK), f32),
            vmem((2, 4, 2, 4, ROWS, D), bf16),
            vmem((2, 4, 4, ROWS, D - S1), bf16),
            vmem((2, 2, 4, 2, ROWS, D // 2), bf16),
            vmem((2, 2, 4, 2, ROWS, D), bf16),
            vmem((2, 2, 2, ROWS, D // 2), bf16),
            vmem((2, 2, 2, ROWS, D), bf16),
            vmem((2, ROWS, S1), bf16),
            vmem((FF, 256), f32),
            vmem((FF, 256), f32),
            vmem((FF, 256), bf16),
            vmem((2, FF, 256), bf16),
            vmem((2, 256, FF), bf16),
            vmem((256, RANK), bf16),
            vmem((FF, RANK), f32),
            vmem((FF, RANK), bf16),
            vmem((2, FF, UT), bf16),
            dma((2, 2)),
            dma((5,)),
            dma((2,)),
            {k: dma(v) for k, v in SEMAPHORES.items()},
            {k: dma(v) for k, v in SEMAPHORES.items()},
        ],
        compiler_params=pltpu.CompilerParams(
            collective_id=0, has_side_effects=True, vmem_limit_bytes=63 * 2**20
        ),
    )(*args)


def solution(mesh):
    rows = P("pipe", ("tensor", "dp"), None)
    return jax.shard_map(
        per_device,
        mesh=mesh,
        in_specs=(rows, rows, P("pipe", None, ("tensor", "dp"), None), rows, P("pipe", None, None), rows, rows),
        out_specs=(rows, rows),
        check_vma=False,
    )
```

```python
import functools

import jax
import jax.numpy as jnp
from jax import lax
from jax.experimental import pallas as pl
from jax.experimental.pallas import tpu as pltpu
from jax.sharding import PartitionSpec as P

beta_one = 0.9
beta_two = 0.999
bias_one = 1.0 - 0.9**10
bias_two = 1.0 - 0.999**10
epsilon = 1e-08

MESH = pl.DeviceIdType.MESH
bf16, f32 = jnp.bfloat16, jnp.float32
D, FF, RANK = 4096, 448, 512
ROWS = 16
C1 = 2816
S1 = 3072
CT = 1024
UT = 1024
NT = (((1,), (1,)), ((), ()))
NN = (((1,), (0,)), ((), ()))
CHUNKS = (0, 2, 1, 3)

KINDS = ("gz", "gm", "gmo", "gl", "glo", "gy", "ry", "rlo", "rl", "rmo", "rm", "rz", "out")
ORDER = (
    (2, 1, 0, 0), (2, 1, 0, 1), (2, 0, 0, 1), (2, 0, 0, 0), (1, 0), (4, 0, 0, 0, 0), (4, 0, 0, 0, 1),
    (4, 1, 0, 0, 1), (4, 1, 0, 0, 0), (1, 1), (0, 1, 1, 0, 0), (3, 1, 0, 0), (0, 1, 1, 0, 1), (3, 1, 0, 1),
    (0, 1, 0, 0, 1), (3, 0, 0, 1), (0, 0, 0), (2, 0, 1, 0), (6, 0, 0, 1), (0, 1, 0, 0, 0), (6, 0, 0, 3),
    (4, 0, 1, 0, 0), (4, 0, 1, 0, 1), (2, 0, 1, 1), (6, 1, 0, 1), (3, 0, 0, 0), (6, 1, 0, 3), (0, 0, 1),
    (2, 1, 1, 0), (2, 1, 1, 1), (4, 1, 1, 0, 1), (4, 1, 1, 0, 0), (0, 3, 0, 0, 0, 0), (6, 0, 3, 0),
    (0, 3, 1, 0, 0, 0), (6, 1, 3, 0), (5, 0, 0, 0, 0), (0, 3, 0, 0, 0, 1), (5, 0, 0, 0, 1),
    (0, 3, 1, 0, 0, 1), (5, 1, 0, 0, 1), (0, 1, 0, 1, 0), (3, 0, 1, 0), (6, 0, 1, 0), (6, 1, 1, 0),
    (5, 1, 0, 0, 0), (0, 3, 0, 1, 0, 0), (5, 0, 1, 0, 0), (0, 3, 0, 1, 0, 1), (5, 0, 1, 0, 1),
    (0, 1, 0, 1, 1), (3, 0, 1, 1), (0, 2, 0, 0), (6, 0, 0, 2), (4, 0, 0, 2, 0), (4, 0, 0, 2, 1),
    (0, 2, 1, 0), (4, 1, 0, 2, 1), (4, 1, 0, 2, 0), (6, 1, 0, 2), (0, 4, 0, 0, 0), (6, 0, 2, 0),
    (0, 1, 1, 1, 0), (3, 1, 1, 0), (0, 1, 1, 1, 1), (3, 1, 1, 1), (0, 4, 1, 0, 0), (6, 1, 2, 0),
    (0, 3, 1, 1, 0, 0), (5, 1, 1, 0, 0), (0, 3, 1, 1, 0, 1), (5, 1, 1, 0, 1), (0, 2, 0, 1), (4, 0, 1, 2, 0),
    (4, 0, 1, 2, 1), (4, 1, 0, 1, 1), (4, 1, 0, 1, 0), (0, 3, 0, 0, 2, 0), (6, 0, 3, 2), (0, 3, 0, 0, 2, 1),
    (6, 0, 1, 2), (5, 0, 0, 2, 0), (5, 0, 0, 2, 1), (0, 3, 1, 0, 2, 1), (6, 1, 1, 2), (0, 5, 0, 0),
    (0, 4, 0, 1, 0), (0, 5, 1, 0), (0, 4, 1, 1, 0), (7, 0), (4, 0, 0, 1, 0), (0, 2, 1, 1), (4, 1, 1, 2, 1),
    (4, 1, 1, 2, 0), (4, 0, 0, 1, 1), (8, 0), (0, 3, 1, 0, 2, 0), (6, 1, 3, 2), (9, 0), (10, 0),
    (5, 1, 0, 2, 1), (5, 1, 0, 2, 0), (12, 0, 0), (12, 0, 1), (12, 0, 2), (0, 3, 1, 0, 1, 0), (6, 1, 3, 1),
    (0, 3, 1, 0, 1, 1), (6, 1, 1, 1), (12, 0, 3), (0, 3, 0, 1, 2, 0), (5, 0, 1, 2, 0), (0, 3, 0, 1, 2, 1),
    (5, 0, 1, 2, 1), (4, 1, 1, 1, 0), (5, 1, 0, 1, 1), (11, 0), (0, 4, 0, 0, 2), (6, 0, 2, 2),
    (4, 0, 1, 1, 0), (4, 0, 1, 1, 1), (0, 3, 1, 1, 2, 1), (5, 1, 1, 2, 1), (13, 0, 1, 0), (13, 0, 2, 0),
    (0, 3, 1, 1, 2, 0), (5, 1, 1, 2, 0), (13, 0, 0, 0), (4, 1, 1, 1, 1), (13, 0, 3, 0), (0, 4, 1, 0, 2),
    (6, 1, 2, 2), (0, 3, 0, 0, 1, 0), (5, 0, 0, 1, 0), (0, 3, 0, 0, 1, 1), (5, 0, 0, 1, 1), (5, 1, 0, 1, 0),
    (6, 0, 3, 1), (4, 0, 0, 3, 0), (4, 0, 0, 3, 1), (4, 1, 0, 3, 1), (4, 1, 0, 3, 0), (6, 0, 1, 1),
    (13, 1, 0, 0), (0, 6, 0, 0), (14, 0, 2, 0), (14, 0, 0, 0), (14, 0, 1, 0), (14, 0, 3, 0), (13, 1, 1, 0),
    (13, 1, 3, 0), (0, 5, 0, 2), (0, 4, 0, 1, 2), (0, 5, 1, 2), (0, 4, 1, 1, 2), (7, 2), (13, 1, 2, 0),
    (8, 2), (0, 4, 0, 0, 1), (6, 0, 2, 1), (0, 3, 0, 1, 1, 0), (5, 0, 1, 1, 0), (0, 3, 0, 1, 1, 1),
    (5, 0, 1, 1, 1), (0, 3, 1, 1, 1, 0), (5, 1, 1, 1, 0), (0, 3, 1, 1, 1, 1), (5, 1, 1, 1, 1), (9, 2),
    (0, 4, 1, 0, 1), (6, 1, 2, 1), (4, 1, 1, 3, 0), (4, 0, 1, 3, 0), (4, 1, 1, 3, 1), (4, 0, 1, 3, 1),
    (10, 2), (12, 2, 0), (12, 2, 1), (12, 2, 2), (12, 2, 3), (0, 3, 0, 0, 3, 0), (5, 0, 0, 3, 0),
    (6, 0, 3, 3), (13, 0, 3, 2), (0, 3, 0, 0, 3, 1), (5, 0, 0, 3, 1), (0, 3, 1, 0, 3, 0), (5, 1, 0, 3, 0),
    (0, 3, 1, 0, 3, 1), (5, 1, 0, 3, 1), (0, 6, 1, 0), (14, 1, 1, 0), (14, 1, 2, 0), (14, 1, 0, 0),
    (14, 1, 3, 0), (13, 0, 0, 2), (11, 2), (13, 0, 1, 2), (13, 0, 2, 2), (6, 1, 3, 3), (15, 0, 1, 2, 0),
    (15, 0, 1, 0, 1), (15, 1, 1, 0, 1), (15, 1, 1, 0, 0), (0, 5, 0, 1), (0, 4, 0, 1, 1), (0, 5, 1, 1),
    (0, 4, 1, 1, 1), (7, 1), (15, 0, 1, 0, 0), (15, 1, 0, 0, 0), (15, 0, 0, 0, 1), (15, 1, 1, 2, 1), (8, 1),
    (6, 0, 1, 3), (15, 0, 0, 0, 0), (15, 1, 0, 0, 1), (9, 1), (0, 3, 0, 1, 3, 0), (5, 0, 1, 3, 0),
    (0, 3, 1, 1, 3, 0), (5, 1, 1, 3, 0), (0, 3, 0, 1, 3, 1), (5, 0, 1, 3, 1), (0, 3, 1, 1, 3, 1),
    (5, 1, 1, 3, 1), (6, 1, 1, 3), (10, 1), (12, 1, 0), (15, 1, 1, 2, 0), (15, 0, 1, 2, 1), (12, 1, 1),
    (0, 4, 1, 0, 3), (6, 1, 2, 3), (15, 0, 1, 1, 0), (15, 1, 1, 1, 0), (0, 6, 0, 2), (14, 0, 1, 2),
    (14, 0, 3, 2), (14, 0, 2, 2), (15, 0, 0, 2, 1), (14, 0, 0, 2), (12, 1, 2), (0, 4, 0, 0, 3), (6, 0, 2, 3),
    (15, 1, 0, 1, 0), (15, 0, 0, 1, 0), (15, 0, 1, 1, 1), (15, 1, 1, 1, 1), (0, 7, 1, 1, 0, 0),
    (16, 1, 1, 0, 0), (0, 7, 0, 1, 0, 1), (16, 0, 1, 0, 1), (0, 7, 1, 1, 0, 1), (16, 1, 1, 0, 1),
    (17, 1, 1, 0, 1), (0, 7, 0, 1, 0, 0), (16, 0, 1, 0, 0), (0, 7, 0, 1, 2, 0), (16, 0, 1, 2, 0),
    (17, 0, 1, 0, 1), (17, 0, 1, 2, 0), (17, 1, 1, 0, 0), (0, 7, 0, 0, 0, 1), (16, 0, 0, 0, 1),
    (0, 7, 1, 0, 0, 0), (16, 1, 0, 0, 0), (0, 7, 1, 1, 2, 1), (16, 1, 1, 2, 1), (12, 1, 3), (13, 0, 0, 1),
    (17, 1, 1, 2, 1), (0, 7, 0, 0, 0, 0), (16, 0, 0, 0, 0), (13, 0, 3, 1), (11, 1), (17, 0, 0, 0, 1),
    (13, 0, 1, 1), (13, 0, 2, 1), (17, 0, 1, 0, 0), (15, 1, 0, 2, 0), (0, 7, 1, 0, 0, 1), (16, 1, 0, 0, 1),
    (17, 1, 0, 0, 1), (0, 7, 0, 1, 2, 1), (16, 0, 1, 2, 1), (17, 1, 0, 0, 0), (0, 7, 1, 1, 2, 0),
    (16, 1, 1, 2, 0), (13, 1, 0, 2), (0, 7, 0, 1, 1, 0), (16, 0, 1, 1, 0), (17, 0, 1, 1, 0),
    (0, 7, 1, 1, 1, 0), (16, 1, 1, 1, 0), (13, 1, 3, 2), (0, 7, 1, 1, 1, 1), (16, 1, 1, 1, 1),
    (0, 7, 0, 0, 2, 1), (16, 0, 0, 2, 1), (17, 0, 1, 2, 1), (13, 1, 2, 2), (0, 7, 0, 1, 1, 1),
    (16, 0, 1, 1, 1), (17, 1, 1, 1, 1), (13, 1, 1, 2), (15, 0, 0, 2, 0), (17, 1, 1, 2, 0), (0, 5, 0, 3),
    (0, 4, 0, 1, 3), (0, 5, 1, 3), (0, 4, 1, 1, 3), (7, 3), (17, 0, 1, 1, 1), (13, 1, 1, 1), (13, 1, 3, 1),
    (8, 3), (17, 0, 0, 0, 0), (17, 1, 1, 1, 0), (13, 1, 2, 1), (13, 1, 0, 1), (0, 8, 1, 1, 0), (18, 1, 1, 0),
    (9, 3), (17, 0, 0, 2, 1), (0, 6, 0, 1), (14, 0, 1, 1), (0, 7, 0, 0, 1, 0), (16, 0, 0, 1, 0),
    (17, 0, 0, 1, 0), (14, 0, 2, 1), (14, 0, 0, 1), (14, 0, 3, 1), (0, 8, 0, 1, 0), (18, 0, 1, 0), (10, 3),
    (12, 3, 0), (15, 0, 0, 1, 1), (0, 8, 1, 0, 0), (18, 1, 0, 0), (0, 6, 1, 2), (14, 1, 3, 2), (14, 1, 0, 2),
    (14, 1, 1, 2), (0, 7, 1, 0, 2, 0), (16, 1, 0, 2, 0), (17, 1, 0, 2, 0), (14, 1, 2, 2), (15, 1, 0, 2, 1),
    (0, 7, 0, 0, 2, 0), (16, 0, 0, 2, 0), (17, 0, 0, 2, 0), (0, 8, 0, 1, 2), (18, 0, 1, 2), (19, 0, 1, 1),
    (12, 3, 1), (19, 0, 1, 0), (0, 8, 1, 1, 2), (18, 1, 1, 2), (19, 1, 1, 1), (0, 8, 0, 1, 1), (18, 0, 1, 1),
    (15, 1, 1, 3, 0), (0, 6, 1, 1), (14, 1, 1, 1), (0, 7, 1, 0, 1, 0), (16, 1, 0, 1, 0), (14, 1, 3, 1),
    (14, 1, 2, 1), (15, 1, 0, 1, 1), (14, 1, 0, 1), (12, 3, 2), (15, 0, 1, 3, 0), (15, 0, 1, 3, 1),
    (15, 1, 0, 3, 0), (15, 1, 1, 3, 1), (0, 8, 0, 0, 0), (18, 0, 0, 0), (19, 1, 1, 0), (0, 8, 1, 1, 1),
    (18, 1, 1, 1), (12, 3, 3), (13, 0, 0, 3), (13, 0, 1, 3), (13, 0, 3, 3), (15, 0, 0, 3, 0),
    (17, 1, 0, 1, 0), (11, 3), (13, 0, 2, 3), (13, 1, 1, 3), (13, 1, 0, 3), (0, 7, 0, 0, 1, 1),
    (16, 0, 0, 1, 1), (17, 0, 0, 1, 1), (0, 7, 1, 0, 2, 1), (16, 1, 0, 2, 1), (17, 1, 0, 2, 1), (27,),
    (13, 1, 3, 3), (13, 1, 2, 3), (0, 7, 1, 0, 1, 1), (16, 1, 0, 1, 1), (17, 1, 0, 1, 1), (0, 7, 1, 1, 3, 0),
    (16, 1, 1, 3, 0), (17, 1, 1, 3, 0), (0, 7, 0, 1, 3, 1), (16, 0, 1, 3, 1), (17, 0, 1, 3, 1),
    (0, 7, 0, 1, 3, 0), (16, 0, 1, 3, 0), (17, 0, 1, 3, 0), (0, 7, 1, 1, 3, 1), (16, 1, 1, 3, 1),
    (0, 9, 0, 1, 0), (20, 0, 1, 0), (21, 0, 1, 0), (0, 8, 0, 0, 2), (18, 0, 0, 2), (0, 9, 1, 1, 0),
    (20, 1, 1, 0), (21, 1, 1, 0), (28, 0), (17, 1, 1, 3, 1), (0, 6, 0, 3), (14, 0, 2, 3), (19, 0, 0, 0),
    (15, 0, 0, 3, 1), (14, 0, 3, 3), (14, 0, 0, 3), (14, 0, 1, 3), (0, 7, 0, 0, 3, 0), (16, 0, 0, 3, 0),
    (17, 0, 0, 3, 0), (28, 1), (19, 0, 0, 1), (0, 8, 0, 0, 1), (18, 0, 0, 1), (0, 8, 1, 0, 2), (18, 1, 0, 2),
    (19, 1, 0, 1), (28, 2), (19, 1, 0, 0), (0, 6, 1, 3), (14, 1, 1, 3), (0, 7, 1, 0, 3, 0), (16, 1, 0, 3, 0),
    (17, 1, 0, 3, 0), (14, 1, 2, 3), (15, 1, 0, 3, 1), (28, 3), (0, 8, 0, 1, 3), (18, 0, 1, 3),
    (0, 7, 0, 0, 3, 1), (16, 0, 0, 3, 1), (17, 0, 0, 3, 1), (14, 1, 3, 3), (14, 1, 0, 3), (0, 9, 0, 1, 1),
    (20, 0, 1, 1), (21, 0, 1, 1), (0, 8, 1, 0, 1), (18, 1, 0, 1), (0, 8, 1, 1, 3), (18, 1, 1, 3),
    (0, 9, 1, 1, 1), (20, 1, 1, 1), (21, 1, 1, 1), (0, 9, 0, 0, 0), (20, 0, 0, 0), (21, 0, 0, 0),
    (0, 7, 1, 0, 3, 1), (16, 1, 0, 3, 1), (17, 1, 0, 3, 1), (0, 9, 1, 0, 0), (20, 1, 0, 0), (21, 1, 0, 0),
    (0, 10, 0, 1), (22, 0, 1), (23, 0), (0, 8, 0, 0, 3), (18, 0, 0, 3), (0, 9, 0, 0, 1), (20, 0, 0, 1),
    (21, 0, 0, 1), (0, 10, 1, 1), (22, 1, 1), (23, 1), (0, 8, 1, 0, 3), (18, 1, 0, 3), (0, 9, 1, 0, 1),
    (20, 1, 0, 1), (21, 1, 0, 1), (0, 10, 0, 0), (22, 0, 0), (0, 11, 0), (24, 0), (25, 0), (0, 10, 1, 0),
    (22, 1, 0), (0, 11, 1), (24, 1), (25, 1), (0, 12, 0), (0, 12, 1),
)


def dot(a, b, dims=NN):
    return lax.dot_general(a, b, dims, preferred_element_type=f32)


def kernel(tok, grd, win, wdn, prj, mom1, mom2, out_prev, out_upd,
           buf, WI, WD, PR, M1, M2, part, R1, R2o, R2, R3o, R3, R4,
           GA, UA, HI, GT, TA, PC, LG, NM, US,
           lsem, wsem, usem, recv, sent):
    pipe = lax.axis_index("pipe")
    t = lax.axis_index("tensor")
    x = lax.axis_index("dp")
    z0, y = t // 4, t % 4
    z1 = 1 - z0
    Z = (z0, z1)
    L0, M0 = (y, x), (x, y)

    def dev(h, l, m, z):
        return {"tensor": z * 4 + (l if h == 0 else m), "dp": m if h == 0 else l}

    def to(v, d):
        return (v + 1 + 2 * d) % 4

    def ldev(h, d):
        return dev(h, to(L0[h], d), M0[h], z0)

    def mdev(h, d):
        return dev(h, L0[h], to(M0[h], d), z0)

    zdev = dev(0, L0[0], M0[0], z1)
    pdev = {"pipe": (pipe + 3) % 4}
    barrier = pltpu.get_barrier_semaphore()
    for h in (0, 1):
        for d in (0, 1):
            pl.semaphore_signal(barrier, inc=1, device_id=ldev(h, d), device_id_type=MESH)
    pl.semaphore_signal(barrier, inc=1, device_id=zdev, device_id_type=MESH)
    for step in (1, 3):
        pl.semaphore_signal(
            barrier, inc=1, device_id={"pipe": (pipe + step) % 4}, device_id_type=MESH
        )

    own = [
        pltpu.make_async_copy(
            src.at[0, h * ROWS : (h + 1) * ROWS, :],
            buf.at[h, M0[h], L0[h], z0, a],
            lsem.at[h, a],
        )
        for h in (0, 1)
        for a, src in ((0, tok), (1, grd))
    ]
    for c in own:
        c.start()
    loads = [
        pltpu.make_async_copy(src.at[0], dst, wsem.at[i])
        for i, (src, dst) in enumerate(((win, WI), (wdn, WD), (prj, PR), (mom1, M1), (mom2, M2)))
    ]
    for c in loads:
        c.start()
    for c in own:
        c.wait()
    pl.semaphore_wait(barrier, 7)

    def group(key):
        name = key[0]
        if name in ("gmo", "glo", "rl", "rm"):
            return name, key[1:-1]
        if name in ("gy", "ry"):
            return name, (key[1], key[3])
        return name, key[1:]

    def send(src, dst, key, to_dev):
        name, idx = group(key)
        c = pltpu.make_async_remote_copy(
            src,
            dst,
            sent.at[FAMILIES.index(family(key))],
            recv[name].at[idx],
            device_id=to_dev,
            device_id_type=MESH,
        )
        c.start()

    def rot(v, r):
        return (v + r) % 4

    def cols(zz, edge):
        return (0, D) if zz == 0 else (0, edge)

    def half(zz, d, edge):
        n = cols(zz, edge)[1] // 2
        return (0, n) if d == 0 else (n, 2 * n)

    def piece(h, lr, zz, mr, c):
        return buf.at[h, rot(M0[h], mr), rot(L0[h], lr), Z[zz], :, :, c[0] : c[1]]

    def psum(h, lr, zz, mr, c):
        return part.at[h, rot(M0[h], mr), rot(L0[h], lr), Z[zz], :, c[0] : c[1]]

    def landing(key):
        name, h, *rest = key
        if name == "gz":
            return piece(h, 0, 1, 0, (0, D))
        if name == "gm":
            zz, d = rest
            return piece(h, 0, zz, 3 - 2 * d, cols(zz, C1))
        if name == "gmo":
            zz, d = rest
            return piece(h, 0, zz, 2, half(zz, d, C1))
        if name == "gl":
            zz, mr, d = rest
            return piece(h, 3 - 2 * d, zz, mr, cols(zz, C1))
        if name == "glo":
            zz, mr, d = rest
            return piece(h, 2, zz, mr, half(zz, d, C1))
        if name == "gy":
            lr, mr = rest
            return piece(h, lr, 1, mr, (C1, D))
        if name == "ry":
            return R1.at[h, rest[1], rest[0]]
        if name == "rlo":
            zz, mr, d = rest
            return R2o.at[h, zz, mr, d, :, 0 : cols(zz, S1)[1] // 2]
        if name == "rl":
            zz, mr, d = rest
            return R2.at[h, zz, mr, d, :, 0 : cols(zz, S1)[1]]
        if name == "rmo":
            zz, d = rest
            return R3o.at[h, zz, d, :, 0 : cols(zz, S1)[1] // 2]
        if name == "rm":
            zz, d = rest
            return R3.at[h, zz, d, :, 0 : cols(zz, S1)[1]]
        if name == "rz":
            return R4.at[h]
        return out_prev.at[0, h * ROWS : (h + 1) * ROWS, :]

    def arrived(name, h, *rest):
        if name == "gmo":
            return piece(h, 0, rest[0], 2, cols(rest[0], C1))
        if name == "glo":
            return piece(h, 2, rest[0], rest[1], cols(rest[0], C1))
        if name == "gy":
            n = 3 if rest[0] == 0 else 4
            return buf.at[h, rot(M0[h], rest[0]), 0:n, z1, :, :, C1:D]
        if name == "ry":
            return R1.at[h, rest[0]]
        if name == "rl":
            return R2.at[h, rest[0], rest[1], :, :, 0 : cols(rest[0], S1)[1]]
        if name == "rm":
            return R3.at[h, rest[0], :, :, 0 : cols(rest[0], S1)[1]]
        return landing((name, h, *rest))

    def w(kind, *idx):
        name = KINDS[kind]
        ref = arrived(name, *idx)
        pltpu.make_async_remote_copy(
            ref, ref, sent.at[0], recv[name].at[idx], device_id=zdev, device_id_type=MESH
        ).wait_recv()

    def gsend(key, ref, to_dev):
        send(ref, ref, key, to_dev)

    def gz(h):
        gsend(("gz", h), piece(h, 0, 0, 0, (0, D)), zdev)

    def gm(h, zz, d):
        gsend(("gm", h, zz, d), piece(h, 0, zz, 0, cols(zz, C1)), mdev(h, d))

    def gmo(h, zz, d):
        gsend(("gmo", h, zz, d), piece(h, 0, zz, 3 - 2 * d, half(zz, d, C1)), mdev(h, d))

    def gl(h, zz, mr, d):
        gsend(("gl", h, zz, mr, d), piece(h, 0, zz, mr, cols(zz, C1)), ldev(h, d))

    def glo(h, zz, mr, d):
        gsend(("glo", h, zz, mr, d), piece(h, 3 - 2 * d, zz, mr, half(zz, d, C1)), ldev(h, d))

    def gy(h, lr, mr):
        gsend(("gy", h, lr, mr), piece(h, lr, 0, mr, (C1, D)), zdev)

    def rows_of(mr, a):
        return jnp.concatenate(
            [buf[h, rot(M0[h], mr), :, :, a].reshape(8 * ROWS, D) for h in (0, 1)], 0
        )

    def t_gate(mr):
        if mr == CHUNKS[0]:
            for c in loads[:3]:
                c.wait()
        GA[...] = dot(WI[0], rows_of(mr, 0), NT)

    def t_up(mr):
        UA[...] = dot(WI[1], rows_of(mr, 0), NT)

    def t_act(mr):
        gh = dot(WD[...], rows_of(mr, 1), NT)
        g, u = GA[...], UA[...]
        s = 1.0 / (1.0 + jnp.exp(-g))
        silu = g * s
        HI[...] = (silu * u).astype(bf16)
        GT[0] = (gh * u * s * (1.0 + g * (1.0 - s))).astype(bf16)
        GT[1] = (gh * silu).astype(bf16)

    def t_turn(mr):
        TA[0] = GT[0].T
        TA[1] = GT[1].T

    def t_low(mr):
        PC[...] = dot(rows_of(mr, 1), PR[...]).astype(bf16)
        low = dot(HI[...], PC[...])
        LG[...] = low if mr == CHUNKS[0] else LG[...] + low

    def t_in(mr, j):
        c = slice(j * CT, (j + 1) * CT)
        r = (dot(TA[0], WI[0, :, c]) + dot(TA[1], WI[1, :, c])).astype(bf16)
        for h in (0, 1):
            part[h, rot(M0[h], mr), :, :, :, c] = r[h * 128 : (h + 1) * 128].reshape(
                4, 2, ROWS, CT
            )

    def add(dst, *refs):
        total = dst[...].astype(f32)
        for r in refs:
            total += r[...].astype(f32)
        dst[...] = total.astype(bf16)

    def rsend(key, src, to_dev):
        send(src, landing(key), key, to_dev)

    def ry(h, lr, mr):
        rsend(("ry", h, lr, mr), psum(h, lr, 1, mr, (S1, D)), zdev)

    def y_add(h, lr, mr):
        add(psum(h, lr, 0, mr, (S1, D)), landing(("ry", h, lr, mr)))

    def rlo(h, zz, mr, d):
        rsend(("rlo", h, zz, mr, d), psum(h, 2, zz, mr, half(zz, d, S1)), ldev(h, d))

    def lo_add(h, zz, mr, d):
        add(psum(h, 1 + 2 * d, zz, mr, half(zz, d, S1)), landing(("rlo", h, zz, mr, d)))

    def rl(h, zz, mr, d):
        rsend(("rl", h, zz, mr, d), psum(h, 1 + 2 * d, zz, mr, cols(zz, S1)), ldev(h, d))

    def l_add(h, zz, mr):
        add(
            psum(h, 0, zz, mr, cols(zz, S1)),
            landing(("rl", h, zz, mr, 0)),
            landing(("rl", h, zz, mr, 1)),
        )

    def rmo(h, zz, d):
        rsend(("rmo", h, zz, d), psum(h, 0, zz, 2, half(zz, d, S1)), mdev(h, d))

    def mo_add(h, zz, d):
        add(psum(h, 0, zz, 1 + 2 * d, half(zz, d, S1)), landing(("rmo", h, zz, d)))

    def rm(h, zz, d):
        rsend(("rm", h, zz, d), psum(h, 0, zz, 1 + 2 * d, cols(zz, S1)), mdev(h, d))

    def m_add(h, zz):
        add(
            psum(h, 0, zz, 0, cols(zz, S1)),
            landing(("rm", h, zz, 0)),
            landing(("rm", h, zz, 1)),
        )

    def rz(h):
        rsend(("rz", h), psum(h, 0, 1, 0, (0, S1)), zdev)

    def z_add(h):
        add(psum(h, 0, 0, 0, (0, S1)), landing(("rz", h)))

    def out(h):
        rsend(("out", h), psum(h, 0, 0, 0, (0, D)), pdev)

    def adam():
        for c in loads[3:]:
            c.wait()
        low = LG[...]
        first = beta_one * M1[...] + (1.0 - beta_one) * low
        second = beta_two * M2[...] + (1.0 - beta_two) * low * low
        NM[...] = (first / bias_one / (jnp.sqrt(second / bias_two) + epsilon)).astype(bf16)

    def u_copy(j):
        return pltpu.make_async_copy(
            US.at[j % 2], out_upd.at[0, :, j * UT : (j + 1) * UT], usem.at[j % 2]
        )

    def update(j):
        if j >= 2:
            u_copy(j - 2).wait()
        US[j % 2] = dot(NM[...], PR[j * UT : (j + 1) * UT, :], NT).astype(bf16)
        u_copy(j).start()

    steps = (
        w, gz, gm, gmo, gl, glo, gy, t_gate, t_up, t_act, t_turn, t_low, t_in, ry, y_add, rlo, lo_add, rl, l_add,
        rmo, mo_add, rm, m_add, rz, z_add, out, None, adam, update,
    )
    for op, *rest in ORDER:
        steps[op](*rest)
    for j in (2, 3):
        u_copy(j).wait()

    for i, (name, sub) in enumerate(FAMILIES):
        if name in ("gz", "gm", "gmo", "gl", "glo", "gy"):
            n = D - C1 if name == "gy" else cols(sub, C1)[1] // (2 if name[-1] == "o" else 1)
            at = {"gz": (0, 0, 0), "gl": (0, slice(0, 2)), "glo": (0, slice(0, 2))}.get(
                name, (0, 0, slice(0, 4), 0)
            )
            if name == "gy":
                at = (slice(0, 2), slice(0, 4), slice(0, 3), 0) if sub else (slice(0, 2), slice(0, 3), 0, 0)
            ref = buf.at[at + (slice(None),) * (6 - len(at)) + (slice(0, n),)]
        else:
            n = {"ry": D - S1, "rz": S1, "out": D}.get(name) or cols(sub, S1)[1] // (
                2 if name[-1] == "o" else 1
            )
            at = {"ry": (slice(0, 2), slice(0, 4), slice(0, 4), 0), "rl": (0, slice(0, 2)), "rlo": (0, slice(0, 2))}.get(
                name, (0, 0, slice(0, 4), 0) if name[:2] == "rm" else (0, 0, 0)
            )
            ref = part.at[at + (slice(None),) * (5 - len(at)) + (slice(0, n),)]
        pltpu.make_async_remote_copy(
            ref, ref, sent.at[i], recv["gz"].at[0], device_id=zdev, device_id_type=MESH
        ).wait_send()


FAMILIES = [
    ("gz", 0), ("gm", 0), ("gm", 1), ("gmo", 0), ("gmo", 1), ("gl", 0), ("gl", 1), ("glo", 0), ("glo", 1),
    ("gy", 0), ("gy", 1), ("ry", 0), ("rlo", 0), ("rlo", 1), ("rl", 0), ("rl", 1), ("rmo", 0), ("rmo", 1),
    ("rm", 0), ("rm", 1), ("rz", 0), ("out", 0),
]


def family(key):
    name = key[0]
    if name in ("gz", "ry", "rz", "out"):
        return name, 0
    return name, min(key[2], 1)


SEMAPHORES = {"gz": (2,), "gm": (2, 2, 2), "gmo": (2, 2), "gl": (2, 2, 4, 2), "glo": (2, 2, 4), "gy": (2, 4), "ry": (2, 4), "rlo": (2, 2, 4, 2), "rl": (2, 2, 4), "rmo": (2, 2, 2), "rm": (2, 2), "rz": (2,), "out": (2,)}


SETTLE = 7


def settle(prev, upd, out_prev, out_upd, vp, vu, rsem, wsem):
    n = FF // SETTLE
    trips = [(upd, vu, out_upd, slice(i * n, (i + 1) * n)) for i in range(SETTLE)]
    trips.append((prev, vp, out_prev, slice(0, 2 * ROWS)))
    reads = [
        pltpu.make_async_copy(a.at[0, r], v.at[0, r], rsem.at[i])
        for i, (a, v, _, r) in enumerate(trips)
    ]
    writes = [
        pltpu.make_async_copy(v.at[0, r], o.at[0, r], wsem.at[i])
        for i, (_, v, o, r) in enumerate(trips)
    ]
    for c in reads:
        c.start()
    for a, b in zip(reads, writes):
        a.wait()
        b.start()
    for c in writes:
        c.wait()


def per_device(*args):
    dma = pltpu.SemaphoreType.DMA
    vmem = pltpu.VMEM
    prev, upd = pl.pallas_call(
        kernel,
        out_shape=(
            jax.ShapeDtypeStruct((1, 2 * ROWS, D), bf16),
            jax.ShapeDtypeStruct((1, FF, D), bf16),
        ),
        in_specs=[pl.BlockSpec(memory_space=pl.ANY)] * 7,
        out_specs=[pl.BlockSpec(memory_space=pl.ANY)] * 2,
        scratch_shapes=[
            vmem((2, 4, 4, 2, 2, ROWS, D), bf16),
            vmem((2, FF, D), bf16),
            vmem((FF, D), bf16),
            vmem((D, RANK), bf16),
            vmem((FF, RANK), f32),
            vmem((FF, RANK), f32),
            vmem((2, 4, 4, 2, ROWS, D), bf16),
            vmem((2, 4, 4, ROWS, D - S1), bf16),
            vmem((2, 2, 4, 2, ROWS, D // 2), bf16),
            vmem((2, 2, 4, 2, ROWS, D), bf16),
            vmem((2, 2, 2, ROWS, D // 2), bf16),
            vmem((2, 2, 2, ROWS, D), bf16),
            vmem((2, ROWS, S1), bf16),
            vmem((FF, 256), f32),
            vmem((FF, 256), f32),
            vmem((FF, 256), bf16),
            vmem((2, FF, 256), bf16),
            vmem((2, 256, FF), bf16),
            vmem((256, RANK), bf16),
            vmem((FF, RANK), f32),
            vmem((FF, RANK), bf16),
            vmem((2, FF, UT), bf16),
            dma((2, 2)),
            dma((5,)),
            dma((2,)),
            {k: dma(v) for k, v in SEMAPHORES.items()},
            dma((len(FAMILIES),)),
        ],
        compiler_params=pltpu.CompilerParams(
            collective_id=0, has_side_effects=True, vmem_limit_bytes=63 * 2**20
        ),
    )(*args)
    return pl.pallas_call(
        settle,
        out_shape=(
            jax.ShapeDtypeStruct(prev.shape, bf16),
            jax.ShapeDtypeStruct(upd.shape, bf16),
        ),
        in_specs=[pl.BlockSpec(memory_space=pl.ANY)] * 2,
        out_specs=[pl.BlockSpec(memory_space=pl.ANY)] * 2,
        scratch_shapes=[
            vmem(prev.shape, bf16),
            vmem(upd.shape, bf16),
            dma((SETTLE + 1,)),
            dma((SETTLE + 1,)),
        ],
        compiler_params=pltpu.CompilerParams(vmem_limit_bytes=63 * 2**20),
    )(prev, upd)


def solution(mesh):
    rows = P("pipe", ("tensor", "dp"), None)
    return jax.shard_map(
        per_device,
        mesh=mesh,
        in_specs=(rows, rows, P("pipe", None, ("tensor", "dp"), None), rows, P("pipe", None, None), rows, rows),
        out_specs=(rows, rows),
        check_vma=False,
    )
```
